32 devices in a mesh: fsdp: 4 (over z), col: 8 (over y, x, core).
Axes of the slice: x: 2, y: 2, z: 4, core: 2. Of those that a mesh axis runs over, the one named last changes fastest.
Arguments:
- grad: float32 [8192, 28672], P(('fsdp', 'col')), may hold values from -40 to 40
- basis_old: float32 [8192, 512], P(('fsdp', 'col')), may hold values from -0.0625 to 0.0625
- moment: float32 [512, 28672], P('fsdp', 'col'), may hold values from -6 to 6
Outputs:
- lowrank_grad: float32 [512, 28672], P('fsdp', 'col')
- new_moment: float32 [512, 28672], P('fsdp', 'col')
The draws below stay inside these ranges and needn't reach their ends.
All inputs are finite; a program needn't handle non-finite values.
Results may differ from the reference program's by a relative error of at most 0.017.
Values may be sent and summed in bfloat16 or wider, within the bound.
No kernel may reach another device: no remote copies, remote signals or barrier semaphores. Data moves between devices by JAX's collectives and lax.ppermute only.
A program may use at most 128 MiB of HBM per device.

```python
import math
import jax
import jax.numpy as jnp
from jax import lax

D = 8192
FF = 28672
R = 512
ITERS = 2
NS_STEPS = 5
N_FSDP = 4


def draw_grad(key, part):
    subkeys = jax.random.split(key, 3)
    row_scale = jnp.exp(jax.random.uniform(subkeys[0], (D, 1), jnp.float32) * math.log(10.0))
    col_scale = jnp.exp(jax.random.uniform(subkeys[1], (1, FF), jnp.float32) * math.log(4.0))
    entries = jnp.clip(jax.random.normal(subkeys[2], (D, FF), jnp.float32), -4.0, 4.0)
    return jnp.clip(0.2 * row_scale * col_scale * entries, -40.0, 40.0)


def level_of(own_key, extent, shards, low, largest):
    gain = 1.0
    for axis_at, shards_of in shards:
        draws = jax.random.uniform(jax.random.fold_in(jax.random.fold_in(own_key, 6), axis_at), (shards_of,), jnp.float32, low / len(shards), largest / len(shards))
        gain = gain * jnp.repeat(jnp.exp(draws), extent[axis_at] // shards_of).reshape((-1,) + (1,) * (len(extent) - 1 - axis_at))
    return gain


def centred(stream_key, dims, scale, limit, cuts=(), held_as=jnp.bfloat16):
    factor_of = level_of(stream_key, dims, cuts, -0.22, 0.18) if cuts else 1.0
    values = jax.random.normal(stream_key, dims, jnp.float32) * scale * factor_of
    return jnp.minimum(jnp.maximum(values, -limit), limit).astype(held_as)


def setup_inputs(seed: int = 0) -> dict:
    arg_keys = jax.random.split(jax.random.key(seed), 4)
    return {
        "grad": draw_grad(jax.random.fold_in(arg_keys[3], 71), 0),
        "basis_old": centred(arg_keys[1], (D, R), D ** -0.5, 0.0625, ((0, 32),), jnp.float32),
        "moment": centred(arg_keys[2], (R, FF), 1.0, 6.0, ((0, 4), (1, 8)), jnp.float32),
    }


schulz_a = 3.4445
schulz_b = -4.775
schulz_c = 2.0315

def orthonormal(image):
    highest = lax.Precision.HIGHEST
    scale = jnp.sum(image * image)
    ortho = image / jnp.sqrt(scale)
    for schulz_step in range(NS_STEPS):
        gram = jnp.dot(ortho.T, ortho, precision=highest)
        poly = schulz_b * gram + schulz_c * jnp.dot(gram, gram, precision=highest)
        ortho = schulz_a * ortho + jnp.dot(ortho, poly, precision=highest)
    return ortho

def reference(grad, basis_old, moment):
    highest = lax.Precision.HIGHEST
    grad_half = grad.astype(jnp.bfloat16)
    grad_blocks = grad_half.reshape(N_FSDP, D // N_FSDP, FF)
    basis = basis_old
    for iteration in range(ITERS):
        basis_half = basis.astype(jnp.bfloat16)
        basis_blocks = basis_half.reshape(N_FSDP, D // N_FSDP, R)

        def add_block(running, pair):
            block_grad, block_basis = pair
            term = lax.dot_general(block_grad, block_basis, (((0,), (0,)), ((), ())), preferred_element_type=jnp.float32)
            term = lax.optimization_barrier(term.astype(jnp.bfloat16))
            return (running + term.astype(jnp.float32), None)
        summed, unused = lax.scan(add_block, jnp.zeros((FF, R), jnp.float32), (grad_blocks, basis_blocks))
        coeff = summed.astype(jnp.bfloat16)
        image = jnp.dot(grad_half, coeff, preferred_element_type=jnp.float32)
        basis = orthonormal(image)
    lowrank_grad = lax.dot_general(basis.astype(jnp.bfloat16), grad_half, (((0,), (0,)), ((), ())), preferred_element_type=jnp.float32)
    margin = jnp.dot(basis.T, basis_old, precision=highest)
    new_moment = jnp.dot(margin, moment, precision=highest)
    return (lowrank_grad, new_moment)
```

```python
import jax
import jax.numpy as jnp
from jax import lax
from jax.experimental import pallas as pl
from jax.experimental.pallas import tpu as pltpu
from jax.sharding import PartitionSpec as P

ITERS = 2
NS_STEPS = 5

schulz_a = 3.4445
schulz_b = -4.775
schulz_c = 2.0315

BF = jnp.bfloat16
F32 = jnp.float32
HI = lax.Precision.HIGHEST


def bits_of(count):
    assert count & (count - 1) == 0
    return [1 << b for b in range(count.bit_length() - 1)]


def swap(value, axis, mask):
    count = lax.axis_size(axis)
    return lax.ppermute(value, axis, [(i, i ^ mask) for i in range(count)])


def piece_order(count):
    bits = bits_of(count)
    order = [0]
    for bit in bits[1:][::-1] + bits[:1]:
        order = order + [mask ^ bit for mask in order]
    return order


def reorder(value, have, want):
    if have == want:
        return value
    return jnp.concatenate([value[have.index(m)][None] for m in want], axis=0)


def col_sum_scatter(stack):
    count = stack.shape[0]
    bits = bits_of(count)
    order = piece_order(count)
    half = count // 2
    got = swap(stack[half:], "col", bits[0])
    kept = (stack[:half].astype(F32) + got.astype(F32)).astype(BF)
    width = stack.shape[-1] // 2
    parts = []
    rest = bits[1:]
    for way, sequence in enumerate((rest, rest[1:] + rest[:1])):
        value = kept[:, :, way * width : (way + 1) * width]
        masks = order[:half]
        for bit in sequence:
            stay = [m for m in masks if not m & bit]
            move = [m ^ bit for m in stay]
            mine = reorder(value, masks, stay) if masks[: len(stay)] != stay else value[: len(stay)]
            sent = reorder(value, masks, move) if masks[len(stay) :] != move else value[len(stay) :]
            value = (mine.astype(F32) + swap(sent, "col", bit).astype(F32)).astype(BF)
            masks = stay
        parts.append(value[0])
    return parts


def col_gather(parts):
    count = lax.axis_size("col")
    bits = bits_of(count)
    order = piece_order(count)
    rest = bits[1:]
    sides = []
    for part, sequence in zip(parts, (rest[::-1], (rest[1:] + rest[:1])[::-1])):
        value = part[None]
        masks = [0]
        for bit in sequence:
            value = jnp.concatenate([value, swap(value, "col", bit)], axis=0)
            masks = masks + [m ^ bit for m in masks]
        sides.append(reorder(value, masks, order[: count // 2]))
    near = jnp.concatenate(sides, axis=-1)
    far = swap(near, "col", bits[0])
    return jnp.concatenate([near, far], axis=0).reshape(count * near.shape[1], near.shape[2])


def halves(value):
    width = value.shape[-1] // 2
    return [value[:, :width], value[:, width:]]


def fsdp_sum_small(value):
    for bit in bits_of(lax.axis_size("fsdp")):
        value = value + swap(value, "fsdp", bit)
    return value


def fsdp_sum_line(value):
    if lax.axis_size("fsdp") != 4:
        return lax.psum(value, "fsdp")
    own = lax.axis_index("fsdp")
    middle = (own == 1) | (own == 2)
    got = lax.ppermute(value, "fsdp", [(0, 1), (3, 2)])
    pair = (value.astype(F32) + got.astype(F32)).astype(BF)
    other = lax.ppermute(pair, "fsdp", [(1, 2), (2, 1)])
    total = (pair.astype(F32) + other.astype(F32)).astype(BF)
    back = lax.ppermute(total, "fsdp", [(1, 0), (2, 3)])
    return jnp.where(middle, total, back)


def natural_rows(me, order, src, dst):
    size = src.shape[0] // len(order)
    for place, mask in enumerate(order):
        start = pl.multiple_of((me ^ mask) * size, size)
        dst[pl.ds(start, size), :] = src[place * size : (place + 1) * size, :]


def dot_hi(a, b):
    return jnp.dot(a, b, precision=HI, preferred_element_type=F32)


def schulz_body(order, me_ref, gram_ref, image_ref, basis_ref, q_ref, g_ref):
    rank = gram_ref.shape[1]
    natural_rows(me_ref[0], order, gram_ref, g_ref)
    gram = g_ref[...]
    diagonal = lax.broadcasted_iota(jnp.int32, (rank, rank), 0) == lax.broadcasted_iota(jnp.int32, (rank, rank), 1)
    scale = jnp.sum(jnp.where(diagonal, gram, 0.0), axis=(0, 1), keepdims=True)
    g_ref[...] = gram / scale
    q_ref[...] = jnp.where(diagonal, 1.0 / jnp.sqrt(scale), 0.0)

    def poly_of(g):
        return schulz_b * g + schulz_c * dot_hi(g, g) + jnp.where(diagonal, schulz_a, 0.0)

    def step(_, carry):
        g = g_ref[...]
        poly = poly_of(g)
        q_ref[...] = dot_hi(q_ref[...], poly)
        g_ref[...] = dot_hi(poly, dot_hi(poly, g))
        return carry

    lax.fori_loop(0, NS_STEPS - 1, step, 0)
    q = dot_hi(q_ref[...], poly_of(g_ref[...]))
    q_ref[...] = q
    high = q.astype(BF)
    low = (q - high.astype(F32)).astype(BF)
    image = image_ref[...]
    basis_ref[...] = (
        jnp.dot(image, high, preferred_element_type=F32) + jnp.dot(image, low, preferred_element_type=F32)
    ).astype(BF)


def schulz(me, gram, image):
    rank = gram.shape[1]
    order = piece_order(lax.axis_size("col"))
    vmem = pl.BlockSpec(memory_space=pltpu.VMEM)
    flops = 2 * rank**3 * 18 * 6 + 4 * image.shape[0] * rank * rank
    return pl.pallas_call(
        lambda *refs: schulz_body(order, *refs),
        out_shape=(
            jax.ShapeDtypeStruct(image.shape, BF),
            jax.ShapeDtypeStruct((rank, rank), F32),
        ),
        in_specs=[pl.BlockSpec(memory_space=pltpu.SMEM), vmem, vmem],
        out_specs=(vmem, vmem),
        scratch_shapes=[pltpu.VMEM((rank, rank), F32)],
        cost_estimate=pl.CostEstimate(flops=flops, bytes_accessed=8 * rank * rank, transcendentals=0),
        name="schulz",
    )(me, gram, image)


def margin_body(order, me_ref, q_ref, cross_ref, out_ref, m_ref):
    natural_rows(me_ref[0], order, cross_ref, m_ref)
    share = out_ref.shape[0]
    start = pl.multiple_of(me_ref[1] * share, share)
    out_ref[...] = dot_hi(q_ref[pl.ds(start, share), :], m_ref[...])


def margin_rows_of(me, q, cross):
    rank = q.shape[0]
    share = rank // lax.axis_size("fsdp")
    order = piece_order(lax.axis_size("col"))
    vmem = pl.BlockSpec(memory_space=pltpu.VMEM)
    return pl.pallas_call(
        lambda *refs: margin_body(order, *refs),
        out_shape=jax.ShapeDtypeStruct((share, rank), F32),
        in_specs=[pl.BlockSpec(memory_space=pltpu.SMEM), vmem, vmem],
        out_specs=vmem,
        scratch_shapes=[pltpu.VMEM((rank, rank), F32)],
        cost_estimate=pl.CostEstimate(flops=12 * share * rank * rank, bytes_accessed=8 * rank * rank, transcendentals=0),
        name="margin",
    )(me, q, cross)


def dot_t(a, b):
    return lax.dot_general(a, b, (((0,), (0,)), ((), ())), preferred_element_type=F32)


def cross_sum(left, right):
    count = lax.axis_size("col")
    whole = dot_t(left, right)
    size = whole.shape[0] // count
    own = lax.dynamic_slice_in_dim(whole, lax.axis_index("col") * size, size, 0)
    return col_gather(halves(fsdp_sum_small(own)))


def chunk_width(width):
    for chunks in (7, 4, 2):
        if width % (128 * chunks) == 0:
            return width // chunks
    return width


def exchange(grad):
    count = lax.axis_size("col")
    me = lax.axis_index("col")
    order = piece_order(count)
    width = grad.shape[1] // count
    chunk = chunk_width(width)
    tiles = []
    arrived = []
    for at in range(0, width, chunk):
        pieces = []
        for mask in order:
            start = (me ^ mask) * width + at
            piece = lax.dynamic_slice(grad, (0, start), (grad.shape[0], chunk)).astype(BF)
            if len(arrived) > 1:
                piece, _ = lax.optimization_barrier((piece, arrived[-2][order.index(mask)]))
            pieces.append(swap(piece, "col", mask) if mask else piece)
        arrived.append(pieces)
        tiles.append(jnp.concatenate(pieces, axis=0))
    return tiles


def local(grad, basis_old, moment):
    count = lax.axis_size("col")
    me = jnp.stack([lax.axis_index("col"), lax.axis_index("fsdp")]).astype(jnp.int32)
    rows, rank = basis_old.shape
    basis_start = col_gather(halves(basis_old.astype(BF)))
    tiles = exchange(grad)
    basis = basis_start
    for iteration in range(ITERS):
        image = None
        for tile in tiles:
            coeff = fsdp_sum_line(dot_t(tile, basis).astype(BF))
            term = jnp.dot(tile, coeff, preferred_element_type=F32)
            image = term if image is None else image + term
        image = col_gather(col_sum_scatter(image.astype(BF).reshape(count, rows, rank)))
        gram = cross_sum(image, image)
        basis, q = schulz(me, gram, image)
    cross = cross_sum(image, basis_start)
    lowrank = jnp.concatenate([dot_t(basis, tile).astype(BF) for tile in tiles], axis=1)
    lowrank = lax.psum_scatter(lowrank, "fsdp", scatter_dimension=0, tiled=True).astype(F32)
    margin_rows = margin_rows_of(me, q, cross)
    moments = lax.all_gather(moment.astype(BF), "fsdp", axis=0, tiled=True).astype(F32)
    new_moment = jnp.dot(margin_rows, moments, precision=HI)
    return (lowrank, new_moment)


def solution(mesh):
    placed = (P(("fsdp", "col"), None), P(("fsdp", "col"), None), P("fsdp", "col"))
    return jax.shard_map(
        local,
        mesh=mesh,
        in_specs=placed,
        out_specs=(P("fsdp", "col"), P("fsdp", "col")),
        check_vma=False,
    )
```
